32 devices in a mesh: grp: 2 (over y), ep: 8 (over z, x), tp: 2 (over core).
Axes of the slice: x: 2, y: 2, z: 4, core: 2. Of those that a mesh axis runs over, the one named last changes fastest.
Arguments:
- queries: bfloat16 [1024, 16, 576], P(('grp', 'ep'), 'tp'), parts along dimension 0, may hold values from -450 to 450
- latent_cache: bfloat16 [48, 512, 576], P(('grp', 'ep'), 'tp'), parts along dimension 0, may hold values from -6 to 6
- residual: bfloat16 [1024, 2048], P(('grp', 'ep')), parts along dimension 0, may hold values from -8 to 8
- token_request: int32 [1024], P(('grp', 'ep')), parts along dimension 0, may hold values from 0 to 2, as said below
- token_visible: int32 [1024], P(('grp', 'ep')), parts along dimension 0, may hold values from 1 to 512, as said below
- value_proj: bfloat16 [16, 512, 128], P('tp', 'ep'), may hold values from -0.25 to 0.25
- out_proj: bfloat16 [2048, 2048], P('tp', 'ep'), may hold values from -0.125 to 0.125
- norm_gain: float32 [2048], replicated, may hold values from 0.1 to 1.9
- router: bfloat16 [2048, 64], replicated, may hold values from -0.0390625 to 0.0390625
- expert_ids: int32 [1024, 6], P(('grp', 'ep')), parts along dimension 0, may hold values from 0 to 63, all different within a row; in each aligned block of 64 rows (0 to 63, 64 to 127, ...) at most 8 rows name the same one
- gate_weight: bfloat16 [128, 2048, 384], P('ep', None, 'tp'), may hold values from -0.125 to 0.125
- up_weight: bfloat16 [128, 2048, 384], P('ep', None, 'tp'), may hold values from -0.125 to 0.125
- down_weight: bfloat16 [128, 384, 2048], P('ep', 'tp'), may hold values from -0.21875 to 0.21875
Outputs:
- hidden: bfloat16 [1024, 2048], P(('grp', 'ep'), 'tp'), parts along dimension 0
- expert_out: bfloat16 [1024, 2048], P(('grp', 'ep'), 'tp'), parts along dimension 0
The draws below stay inside these ranges and needn't reach their ends.
There are 2 independent parts, one for each index of `grp`. The reference program is written for one: setup_inputs(seed, part) draws one part's arguments, and reference() takes and returns one part's arrays. A program takes and returns all parts, laid end to end along the dimension named above; an argument that names none is the same for every part. Nothing has to cross between parts.
Inputs may be any that keep to these rules, and one draw needn't show every extreme that they name: `token_request`: in each ep block, 62 tokens belong to request 0, a prefill span, and each other request has exactly one token; the tokens' order in the block is arbitrary. `token_visible`: the span's tokens read consecutive counts s + 1 to s + 62; 512 is reached in every draw. `expert_ids`: each row names 6 different experts; among the 64 tokens of one ep index no expert is named by more than 8 tokens, and this bound is reached.
All inputs are finite; a program needn't handle non-finite values.
Results may differ from the reference program's by a relative error of at most 0.018.
Values may be sent and summed in bfloat16 or wider, within the bound.
A program may use at most 128 MiB of HBM per device.

```python
import math
import jax
import jax.numpy as jnp
import numpy as np
from jax import lax

D = 2048
HEADS = 16
LATENT = 512
ROPE = 64
VDIM = 128
EXPERTS = 64
TOPK = 6
EXP_HIDDEN = 768
GROUPS = 2
TOK_DEV = 64
REQ_DEV = 3
CACHE_LEN = 512
CAP = 8
PIECES = 128
TOKENS = 512
REQS = 24
N_EP = 8
N_TP = 2


def request_layout(key):
    blocks = TOKENS // TOK_DEV
    prefill = TOK_DEV - REQ_DEV + 1
    streams = jax.random.split(jax.random.fold_in(key, 101), blocks)

    def one_block(stream, block_index):
        first, second, third = jax.random.split(stream, 3)
        ordering = jax.random.permutation(first, TOK_DEV).astype(jnp.int32)
        span_start = jax.random.randint(second, (), 0, CACHE_LEN - prefill + 1)
        lengths = jax.random.randint(third, (REQ_DEV - 1,), 1, CACHE_LEN + 1)
        lengths = jnp.where((block_index == 0) & (jnp.arange(REQ_DEV - 1) == 0), CACHE_LEN, lengths)
        in_span = ordering < prefill
        request = jnp.where(in_span, 0, ordering - prefill + 1)
        decode_index = jnp.clip(ordering - prefill, 0, REQ_DEV - 2)
        visible = jnp.where(in_span, span_start + ordering + 1, lengths[decode_index])
        return (request.astype(jnp.int32), visible.astype(jnp.int32))
    request, visible = jax.vmap(one_block)(streams, jnp.arange(blocks))
    return (request.reshape(TOKENS), visible.reshape(TOKENS))


def draw_token_request(key, part):
    return request_layout(key)[0]


def draw_token_visible(key, part):
    return request_layout(key)[1]


def cache_rope(key):
    return jnp.clip(jax.random.normal(jax.random.fold_in(key, 202), (REQS, CACHE_LEN, ROPE)), -4.0, 4.0)


def draw_latent_cache(key, part):
    latent = jnp.clip(jax.random.normal(jax.random.fold_in(key, 201), (REQS, CACHE_LEN, LATENT)), -4.0, 4.0)
    return jnp.concatenate([latent, cache_rope(key)], axis=2).astype(jnp.bfloat16)


def draw_queries(key, part):
    shape = (TOKENS, HEADS, LATENT + ROPE)
    values = 0.6 * jnp.clip(jax.random.normal(jax.random.fold_in(key, 301), shape), -4.0, 4.0)
    return values.astype(jnp.bfloat16)


def draw_residual(key, part):
    scales = jnp.exp(jax.random.uniform(jax.random.fold_in(key, 401), (TOKENS, 1), minval=jnp.log(0.2), maxval=jnp.log(2.0)))
    noise = jnp.clip(jax.random.normal(jax.random.fold_in(key, 402), (TOKENS, D)), -4.0, 4.0)
    return (scales * noise).astype(jnp.bfloat16)


def steps_of(own_key, extent, pieces, least, top_value):
    def one(dim, shards_of):
        heights = jax.random.uniform(jax.random.fold_in(jax.random.fold_in(own_key, 6), dim), (shards_of,), jnp.float32, least / len(pieces), top_value / len(pieces))
        return jnp.repeat(jnp.exp(heights), extent[dim] // shards_of).reshape((-1,) + (1,) * (len(extent) - dim - 1))

    level = one(*pieces[0])
    for cut in pieces[1:]:
        level = level * one(*cut)
    return level


def deal_out(stream_key, own, number, rows, count, top, most, skew):
    order = jax.random.permutation(stream_key, count)
    heavy_load, usual = portions_of(count, rows * top, most, skew, True), portions_of(count, rows * top, most, skew, False)
    places = jnp.arange(count)

    def named(tallies, offset_by):
        used = int((tallies > 0).sum())
        fixed = max(1, used // 4)
        moved = fixed + (places - fixed + offset_by * (used - fixed)) % max(1, count - fixed)
        return jnp.zeros((count,), jnp.int32).at[order[jnp.where(places < fixed, places, moved)]].set(jnp.asarray(tallies, jnp.int32))

    tallies = jnp.where(number % 4 == 0, named(heavy_load, number // 4), named(usual, number - number // 4 - 1))
    mixed = jax.random.permutation(jax.random.fold_in(own, 3), count)
    source_of, taker = mixed[0:count // 2 * 2:2], mixed[1:count // 2 * 2:2]
    margin = jnp.minimum(tallies[source_of] - 1, most - tallies[taker]) // 2
    margin = jnp.where((source_of == order[0]) | (taker == order[0]) | (tallies[taker] == 0), 0, jnp.maximum(margin, 0))
    moved = jax.random.randint(jax.random.fold_in(own, 4), (count // 2,), 0, 1 << 20) % (margin + 1)
    tallies = tallies.at[source_of].add(-moved).at[taker].add(moved)
    items = jnp.searchsorted(jnp.cumsum(tallies), jnp.arange(rows * top), side="right").astype(jnp.int32)
    grid = items.reshape(top, rows).T
    grid = grid[jax.random.permutation(jax.random.fold_in(own, 1), rows)]
    offset_by = jax.random.randint(jax.random.fold_in(own, 2), (rows, 1), 0, top)
    return jnp.take_along_axis(grid, (jnp.arange(top)[None, :] + offset_by) % top, axis=1)


def portions_of(amount, total, reach, lean, full):
    loads = [(1 << 20) // math.isqrt(grade ** lean) + 1 for grade in range(1, amount + 1)]
    largest = reach if full else min(reach, max(-(-total // amount), total * loads[0] // sum(loads)))
    least = 1 if total - largest >= amount - 1 else 0
    given, surplus = [largest] + [least] * (amount - 1), total - largest - least * (amount - 1)
    while surplus > 0:
        movable = [i for i in range(1, amount) if given[i] < largest] or [i for i in range(1, amount) if given[i] < reach]
        mass, remaining = sum([loads[i] for i in movable]), surplus
        for i in movable:
            more = min(reach - given[i], max(1, remaining * loads[i] // mass), surplus)
            given[i] = given[i] + more
            surplus = surplus - more
    return np.array(given)


def bell_draw(stream_key, shape, width, most, cuts=(), held_as=jnp.bfloat16):
    gain = steps_of(stream_key, shape, cuts, -0.22, 0.18) if cuts else 1.0
    array = jax.random.normal(stream_key, shape, jnp.float32) * width * gain
    return jnp.minimum(jnp.maximum(array, -most), most).astype(held_as)


def setup_inputs(seed: int = 0, part: int = 0) -> dict:
    key_of = jax.random.split(jax.random.key(seed), 14)
    part_keys = jax.random.split(jax.random.fold_in(key_of[13], part), 14)
    queries = draw_queries(jax.random.fold_in(jax.random.fold_in(key_of[13], part), 71), part)
    latent_cache = draw_latent_cache(jax.random.fold_in(jax.random.fold_in(key_of[13], part), 71), part)
    residual = draw_residual(jax.random.fold_in(jax.random.fold_in(key_of[13], part), 71), part)
    token_request = draw_token_request(jax.random.fold_in(jax.random.fold_in(key_of[13], part), 71), part)
    token_visible = draw_token_visible(jax.random.fold_in(jax.random.fold_in(key_of[13], part), 71), part)
    value_proj = bell_draw(key_of[5], (HEADS, LATENT, VDIM), LATENT ** -0.5, 0.25, ((0, 2), (1, 8)))
    out_proj = bell_draw(key_of[6], (HEADS * VDIM, D), (HEADS * VDIM) ** -0.5, 0.125, ((0, 2), (1, 8)))
    norm_gain = jnp.clip(1.0 + 0.18 * jax.random.normal(key_of[7], (D,), jnp.float32), 0.1, 1.9)
    router = bell_draw(key_of[8], (D, EXPERTS), (12 * D) ** -0.5, 0.0390625)
    expert_ids_keys = jax.random.split(jax.random.fold_in(part_keys[9], 1), TOKENS // TOK_DEV)
    expert_ids_turns = jax.random.permutation(jax.random.fold_in(part_keys[9], 3), TOKENS // TOK_DEV)
    expert_ids = jax.vmap(lambda own, number: deal_out(jax.random.fold_in(part_keys[9], 2), own, number, TOK_DEV, EXPERTS, TOPK, CAP, 2))(expert_ids_keys, expert_ids_turns).reshape((TOKENS, TOPK))
    gate_weight = bell_draw(key_of[10], (PIECES, D, EXP_HIDDEN // GROUPS), D ** -0.5, 0.125, ((0, 8), (2, 2)))
    up_weight = bell_draw(key_of[11], (PIECES, D, EXP_HIDDEN // GROUPS), D ** -0.5, 0.125, ((0, 8), (2, 2)))
    down_weight = bell_draw(key_of[12], (PIECES, EXP_HIDDEN // GROUPS, D), EXP_HIDDEN ** -0.5, 0.21875, ((0, 8), (1, 2)))
    return {"queries": queries, "latent_cache": latent_cache, "residual": residual, "token_request": token_request, "token_visible": token_visible, "value_proj": value_proj, "out_proj": out_proj, "norm_gain": norm_gain, "router": router, "expert_ids": expert_ids, "gate_weight": gate_weight, "up_weight": up_weight, "down_weight": down_weight}


score_scale = 192.0 ** (-0.5)
epsilon = 1e-06

def attend_block(arrays):
    queries, block_rows, token_request, token_visible = arrays
    per_request = block_rows.shape[1]
    flat_rows = block_rows.reshape(-1, block_rows.shape[2]).astype(jnp.float32)
    scores = jnp.einsum('thc,kc->thk', queries.astype(jnp.float32), flat_rows) * score_scale
    column = jnp.arange(flat_rows.shape[0], dtype=jnp.int32)
    owner_id = column // per_request
    position = column % per_request
    allowed = (owner_id[None, :] == token_request[:, None]) & (position[None, :] < token_visible[:, None])
    scores = jnp.where(allowed[:, None, :], scores, -jnp.inf)
    row_peak = lax.optimization_barrier(jnp.max(scores, axis=2, keepdims=True))
    rounded = lax.optimization_barrier(jnp.exp(scores - row_peak).astype(jnp.bfloat16))
    weights = rounded.astype(jnp.float32)
    totals = lax.optimization_barrier(jnp.sum(weights, axis=2, keepdims=True))
    summed = jnp.einsum('thk,kc->thc', weights, flat_rows[:, :LATENT])
    return (summed / totals).astype(jnp.bfloat16)

def reference(queries, latent_cache, residual, token_request, token_visible, value_proj, out_proj, norm_gain, router, expert_ids, gate_weight, up_weight, down_weight):
    blocks = TOKENS // TOK_DEV
    context = lax.map(attend_block, (queries.reshape(blocks, TOK_DEV, HEADS, LATENT + ROPE), latent_cache.reshape(blocks, REQ_DEV, CACHE_LEN, LATENT + ROPE), token_request.reshape(blocks, TOK_DEV), token_visible.reshape(blocks, TOK_DEV)))
    context = context.reshape(TOKENS, HEADS, LATENT)
    heads_out = jnp.einsum('thl,hlv->thv', context.astype(jnp.float32), value_proj.astype(jnp.float32)).astype(jnp.bfloat16)
    heads_out = heads_out.reshape(TOKENS, HEADS * VDIM)
    attention = jnp.dot(heads_out, out_proj, preferred_element_type=jnp.float32)
    hidden = (residual.astype(jnp.float32) + attention).astype(jnp.bfloat16)
    hidden_wide = hidden.astype(jnp.float32)
    normed = (hidden_wide * lax.rsqrt(lax.optimization_barrier(jnp.mean(hidden_wide * hidden_wide, axis=1, keepdims=True)) + epsilon) * norm_gain).astype(jnp.bfloat16)
    logits = jnp.dot(normed, router, preferred_element_type=jnp.float32)
    gate_share = jax.nn.softmax(jnp.take_along_axis(logits, expert_ids, axis=1), axis=1).astype(jnp.bfloat16)
    flat_ids = expert_ids.reshape(-1)
    flat_share = gate_share.reshape(-1).astype(jnp.float32)
    bound = N_EP * CAP
    part_width = EXP_HIDDEN // (GROUPS * N_TP)

    def piece_step(running, piece_index):
        expert = piece_index // GROUPS
        hit_mask = flat_ids == expert
        hits = jnp.nonzero(hit_mask, size=bound, fill_value=0)[0].astype(jnp.int32)
        live = jnp.arange(bound, dtype=jnp.int32) < jnp.sum(hit_mask.astype(jnp.int32))
        token_rows = hits // TOPK
        picked = normed[token_rows]
        gate_vals = jnp.dot(picked, gate_weight[piece_index], preferred_element_type=jnp.float32)
        up_vals = jnp.dot(picked, up_weight[piece_index], preferred_element_type=jnp.float32)
        activated = (jax.nn.silu(gate_vals) * up_vals).astype(jnp.bfloat16)
        combined = jnp.zeros((bound, D), jnp.float32)
        for half_index in range(N_TP):
            lower = half_index * part_width
            piece_out = jnp.dot(activated[:, lower:lower + part_width], down_weight[piece_index, lower:lower + part_width], preferred_element_type=jnp.float32).astype(jnp.bfloat16)
            combined = combined + piece_out.astype(jnp.float32)
        scaled = combined * jnp.where(live, flat_share[hits], 0.0)[:, None]
        return (running.at[token_rows].add(scaled), None)
    routed, _ = lax.scan(piece_step, jnp.zeros((TOKENS, D), jnp.float32), jnp.arange(PIECES, dtype=jnp.int32))
    return (hidden, routed.astype(jnp.bfloat16))
```

```python
import functools

import jax
import jax.numpy as jnp
from jax import lax
from jax.experimental import pallas as pl
from jax.experimental.pallas import tpu as pltpu
from jax.sharding import PartitionSpec as P

LATENT = 512
VDIM = 128
EXPERTS = 64
TOPK = 6
GROUPS = 2
CAP = 8
PIECES = 128
MESH = pl.DeviceIdType.MESH


score_scale = 192.0 ** (-0.5)
epsilon = 1e-06


def masked_scores(queries, block_rows, token_request, token_visible):
    per_request = block_rows.shape[1]
    flat_rows = block_rows.reshape(-1, block_rows.shape[2])
    scores = (
        jnp.einsum("thc,kc->thk", queries, flat_rows, preferred_element_type=jnp.float32)
        * score_scale
    )
    column = jnp.arange(flat_rows.shape[0], dtype=jnp.int32)
    owner_id = column // per_request
    position = column % per_request
    allowed = (owner_id[None, :] == token_request[:, None]) & (
        position[None, :] < token_visible[:, None]
    )
    return (jnp.where(allowed[:, None, :], scores, -jnp.inf), flat_rows)


def weighted_rows(scores, row_peak, flat_rows):
    weights = jnp.exp(scores - row_peak[:, :, None]).astype(jnp.bfloat16)
    totals = jnp.sum(weights.astype(jnp.float32), axis=2)
    summed = jnp.einsum(
        "thk,kc->thc", weights, flat_rows[:, :LATENT], preferred_element_type=jnp.float32
    )
    return (summed, totals)


def expert_block(arrived, gate_weight, up_weight, down_weight):
    gate_vals = jnp.einsum("prd,pdf->prf", arrived, gate_weight, preferred_element_type=jnp.float32)
    up_vals = jnp.einsum("prd,pdf->prf", arrived, up_weight, preferred_element_type=jnp.float32)
    activated = (jax.nn.silu(gate_vals) * up_vals).astype(jnp.bfloat16)
    return jnp.einsum(
        "prf,pfd->prd", activated, down_weight, preferred_element_type=jnp.float32
    ).astype(jnp.bfloat16)


def body(
    queries,
    latent_cache,
    residual,
    token_request,
    token_visible,
    value_proj,
    out_proj,
    norm_gain,
    router,
    expert_ids,
    gate_weight,
    up_weight,
    down_weight,
):
    all_rows = lax.all_gather(latent_cache, "tp", axis=1, tiled=True)
    scores, flat_rows = masked_scores(queries, all_rows, token_request, token_visible)
    summed, totals = weighted_rows(scores, jnp.max(scores, axis=2), flat_rows)
    context = (summed / totals[:, :, None]).astype(jnp.bfloat16)
    tokens_here = context.shape[0]
    heads_here = context.shape[1]
    head_values = jnp.einsum(
        "thl,hlv->thv",
        context,
        lax.all_gather(value_proj, "ep", axis=1, tiled=True),
        preferred_element_type=jnp.float32,
    )
    heads_out = head_values.astype(jnp.bfloat16).reshape(tokens_here, heads_here * VDIM)
    column_block = jnp.dot(
        lax.all_gather(heads_out, "ep", axis=0, tiled=True),
        out_proj,
        preferred_element_type=jnp.float32,
    )
    attention_part = lax.all_to_all(column_block, "ep", split_axis=0, concat_axis=1, tiled=True)
    attention = lax.psum(attention_part, "tp")
    hidden = (residual.astype(jnp.float32) + attention).astype(jnp.bfloat16)
    hidden_wide = hidden.astype(jnp.float32)
    normed = (
        hidden_wide
        * lax.rsqrt(jnp.mean(hidden_wide * hidden_wide, axis=1, keepdims=True) + epsilon)
        * norm_gain
    ).astype(jnp.bfloat16)
    logits = jnp.dot(normed, router, preferred_element_type=jnp.float32)
    gate_share = jax.nn.softmax(jnp.take_along_axis(logits, expert_ids, axis=1), axis=1).astype(
        jnp.bfloat16
    )
    flat_ids = expert_ids.reshape(-1)
    position_id = jnp.arange(flat_ids.shape[0], dtype=jnp.int32)
    earlier = (flat_ids[:, None] == flat_ids[None, :]) & (
        position_id[None, :] < position_id[:, None]
    )
    slot_ids = (flat_ids * CAP + jnp.sum(earlier.astype(jnp.int32), axis=1)).reshape(
        tokens_here, TOPK
    )
    targets = jnp.arange(EXPERTS * CAP, dtype=jnp.int32)
    matches = slot_ids[:, :, None] == targets[None, None, :]
    picker = jnp.any(matches, axis=1).T.astype(jnp.bfloat16)
    model_width = normed.shape[1]
    mixing = jnp.sum(
        jnp.where(matches, gate_share[:, :, None], jnp.zeros((), jnp.bfloat16)), axis=1
    )
    mixing = jnp.broadcast_to(
        mixing.reshape(tokens_here, EXPERTS, 1, CAP), (tokens_here, EXPERTS, GROUPS, CAP)
    ).reshape(tokens_here, PIECES * CAP)
    core_count = lax.axis_size("tp")
    half_width = model_width // core_count
    core_start = lax.axis_index("tp") * half_width
    outgoing = jnp.dot(picker, normed, preferred_element_type=jnp.float32).astype(jnp.bfloat16)
    outgoing = jnp.broadcast_to(
        outgoing.reshape(EXPERTS, 1, CAP, model_width), (EXPERTS, GROUPS, CAP, model_width)
    ).reshape(PIECES, CAP, model_width)
    arrived = lax.all_to_all(outgoing, "ep", split_axis=0, concat_axis=1, tiled=True)
    partial_out = expert_block(arrived, gate_weight, up_weight, down_weight)
    returned = lax.all_to_all(partial_out, "ep", split_axis=1, concat_axis=0, tiled=True)
    routed = jnp.dot(
        mixing, returned.reshape(PIECES * CAP, model_width), preferred_element_type=jnp.float32
    )
    expert_out = lax.psum_scatter(
        routed.astype(jnp.bfloat16), "tp", scatter_dimension=1, tiled=True
    )
    hidden_part = lax.dynamic_slice_in_dim(hidden, core_start, half_width, 1)
    return (hidden_part, expert_out)


def ring_position(index, count):
    half = lax.div(index, 2)
    return half + lax.rem(index, 2) * (count - 1 - 2 * half)


def ring_index(place, count):
    place = lax.rem(place + count, count)
    upper = lax.div(place, count // 2)
    return 2 * place + upper * (2 * count - 1 - 4 * place)


def greet(count):
    me = lax.axis_index("ep")
    core = lax.axis_index("tp")
    barrier = pltpu.get_barrier_semaphore()
    for step in range(1, count):
        pl.semaphore_signal(
            barrier, inc=1, device_id={"ep": lax.rem(me + step, count)}, device_id_type=MESH
        )
    pl.semaphore_signal(barrier, inc=1, device_id={"tp": 1 - core}, device_id_type=MESH)
    pl.semaphore_wait(barrier, count)


def remote(src, dst, send_sem, recv_sem, where):
    return pltpu.make_async_remote_copy(
        src_ref=src,
        dst_ref=dst,
        send_sem=send_sem,
        recv_sem=recv_sem,
        device_id=where,
        device_id_type=MESH,
    )


def ring_gather(count, own, slot, send_sem, recv_sem, arrived):
    me = lax.axis_index("ep")
    place = ring_position(me, count)
    reach = (count // 2, count - 1 - count // 2)
    to = (ring_index(place + 1, count), ring_index(place - 1, count))

    def hop(way, step):
        sign = 1 if way == 0 else -1
        block = ring_index(place - sign * (step - 1), count)
        return remote(
            own if step == 1 else slot(block),
            slot(block),
            send_sem.at[way, step - 1],
            recv_sem.at[way, step - 1],
            {"ep": to[way]},
        )

    hops = {}
    for way in range(2):
        if reach[way] >= 1:
            hops[way, 1] = hop(way, 1)
            hops[way, 1].start()
    arrived(me, 0)
    number = 1
    for step in range(1, reach[0] + 1):
        for way in range(2):
            if step > reach[way]:
                continue
            hops[way, step].wait_recv()
            if step < reach[way]:
                hops[way, step + 1] = hop(way, step + 1)
                hops[way, step + 1].start()
            sign = 1 if way == 0 else -1
            arrived(ring_index(place - sign * step, count), number)
            number += 1
    for copy in hops.values():
        copy.wait_send()


def gather_kernel(
    count, cache_ref, value_ref, ids_ref, rows_ref, values_ref, all_ids_ref,
    tp_send, tp_recv, ring_send, ring_recv, id_send, id_recv, own_sem,
):
    me = lax.axis_index("ep")
    core = lax.axis_index("tp")
    greet(count)
    swap = remote(cache_ref, rows_ref.at[:, core], tp_send, tp_recv, {"tp": 1 - core})
    swap.start()
    owns = [
        pltpu.make_async_copy(cache_ref, rows_ref.at[:, core], own_sem.at[0]),
        pltpu.make_async_copy(value_ref, values_ref.at[:, me], own_sem.at[1]),
        pltpu.make_async_copy(ids_ref, all_ids_ref.at[me], own_sem.at[2]),
    ]
    for copy in owns:
        copy.start()
    id_copies = [
        remote(
            ids_ref, all_ids_ref.at[me], id_send.at[step - 1], id_recv.at[step - 1],
            {"ep": lax.rem(me + step, count)},
        )
        for step in range(1, count)
    ]
    for copy in id_copies:
        copy.start()
    ring_gather(
        count, value_ref, lambda block: values_ref.at[:, block], ring_send, ring_recv,
        lambda block, number: None,
    )
    for copy in id_copies:
        copy.wait()
    for copy in owns:
        copy.wait()
    swap.wait()


def middle_kernel(
    count, heads_ref, proj_ref, residual_ref, gain_ref, normed_ref, hidden_ref,
    gathered, mine, theirs, outbox, inbox, hidden_own, normed_own,
    ring_send, ring_recv, pair_send, pair_recv, back_send, back_recv,
    ring2_send, ring2_recv, fwd_send, fwd_recv, own_sem, swap_send, swap_recv,
):
    me = lax.axis_index("ep")
    core = lax.axis_index("tp")
    tokens = heads_ref.shape[0]
    half = tokens // 2
    width = proj_ref.shape[1]
    model = residual_ref.shape[1]
    greet(count)
    pairs = []

    def project(block, number):
        rows = heads_ref[...] if number == 0 else gathered[block]
        product = jnp.dot(rows, proj_ref[...], preferred_element_type=jnp.float32)
        mine[number] = product.reshape(2, half, width)
        copy = remote(
            mine.at[number, 1 - core], theirs.at[number], pair_send.at[number],
            pair_recv.at[number], {"tp": 1 - core},
        )
        copy.start()
        pairs.append((copy, block))

    backs = []

    def pass_back(number):
        copy, block = pairs[number]
        copy.wait_recv()
        total = (mine[number, core] + theirs[number]).astype(jnp.bfloat16)
        if number == 0:
            inbox[me] = total
        else:
            outbox[number - 1] = total
            back = remote(
                outbox.at[number - 1], inbox.at[me], back_send.at[number - 1],
                back_recv.at[number - 1], {"ep": block},
            )
            back.start()
            backs.append(back)

    def arrived(block, number):
        project(block, number)
        if number >= 1:
            pass_back(number - 1)

    ring_gather(count, heads_ref, lambda block: gathered.at[block], ring_send, ring_recv, arrived)
    pass_back(count - 1)
    for copy, _ in pairs:
        copy.wait_send()
    for back in backs:
        back.wait()
    attention = jnp.concatenate([inbox[i] for i in range(count)], axis=1).astype(jnp.float32)
    hidden = (residual_ref[...].astype(jnp.float32) + attention).astype(jnp.bfloat16)
    wide = hidden.astype(jnp.float32)
    scale = lax.rsqrt(jnp.mean(wide * wide, axis=1, keepdims=True) + epsilon)
    normed_own[...] = (wide * scale * gain_ref[...]).astype(jnp.bfloat16)
    hidden_own[0] = hidden[:, : model // 2]
    hidden_own[1] = hidden[:, model // 2 :]
    swap = remote(
        hidden_own.at[1 - core], hidden_ref.at[core], swap_send, swap_recv, {"tp": 1 - core}
    )
    swap.start()
    owns = [
        pltpu.make_async_copy(hidden_own.at[core], hidden_ref.at[core], own_sem.at[0]),
        pltpu.make_async_copy(normed_own, normed_ref.at[me, core], own_sem.at[1]),
    ]
    for copy in owns:
        copy.start()
    forwards = []

    def forward(block, number):
        source = normed_own if number == 0 else normed_ref.at[block, core]
        copy = remote(
            source, normed_ref.at[block, core], fwd_send.at[number], fwd_recv.at[number],
            {"tp": 1 - core},
        )
        copy.start()
        forwards.append(copy)

    ring_gather(
        count, normed_own, lambda block: normed_ref.at[block, core], ring2_send, ring2_recv, forward
    )
    for copy in forwards:
        copy.wait()
    for copy in owns:
        copy.wait()
    swap.wait()


def return_kernel(
    count, sums_ref, out_ref, theirs, outbox, inbox, pair_send, pair_recv, back_send, back_recv
):
    me = lax.axis_index("ep")
    core = lax.axis_index("tp")
    greet(count)
    order = [lax.rem(me + step, count) for step in list(range(1, count)) + [0]]
    pairs = []
    for number, block in enumerate(order):
        copy = remote(
            sums_ref.at[1 - core, block], theirs.at[number], pair_send.at[number],
            pair_recv.at[number], {"tp": 1 - core},
        )
        copy.start()
        pairs.append(copy)
    backs = []
    for number, block in enumerate(order):
        pairs[number].wait_recv()
        total = sums_ref[core, block].astype(jnp.float32) + theirs[number].astype(jnp.float32)
        if number < count - 1:
            outbox[number] = total.astype(jnp.bfloat16)
            back = remote(
                outbox.at[number], inbox.at[number], back_send.at[number], back_recv.at[number],
                {"ep": block},
            )
            back.start()
            backs.append(back)
    for number, back in enumerate(backs):
        back.wait_recv()
        total = total + inbox[number].astype(jnp.float32)
    out_ref[...] = total.astype(jnp.bfloat16)
    for copy in pairs:
        copy.wait_send()
    for back in backs:
        back.wait_send()


def expert_kernel(blocks, rows_ref, gate_ref, up_ref, down_ref, out_ref):
    rows = rows_ref[0]
    total = None
    for block in range(blocks):
        gate = jnp.dot(rows, gate_ref[block], preferred_element_type=jnp.float32)
        up = jnp.dot(rows, up_ref[block], preferred_element_type=jnp.float32)
        activated = (gate / (1.0 + jnp.exp(-gate)) * up).astype(jnp.bfloat16)
        part = jnp.dot(activated, down_ref[block], preferred_element_type=jnp.float32)
        total = part if total is None else total + part
    out_ref[0] = total.astype(jnp.bfloat16)


def vmem_call(kernel, outs, scratch, ident, *args):
    whole = pl.BlockSpec(memory_space=pltpu.VMEM)
    return pl.pallas_call(
        kernel,
        out_shape=outs,
        in_specs=[whole] * len(args),
        out_specs=jax.tree.map(lambda _: whole, outs),
        scratch_shapes=scratch,
        compiler_params=pltpu.CompilerParams(
            collective_id=ident, has_side_effects=True, vmem_limit_bytes=40 * 2**20
        ),
    )(*args)


def dma(*shape):
    return pltpu.SemaphoreType.DMA(shape)


def lean_body(
    queries,
    latent_cache,
    residual,
    token_request,
    token_visible,
    value_proj,
    out_proj,
    norm_gain,
    router,
    expert_ids,
    gate_weight,
    up_weight,
    down_weight,
):
    count = lax.axis_size("ep")
    core = lax.axis_index("tp")
    me = lax.axis_index("ep")
    tokens, heads = queries.shape[:2]
    half = tokens // 2
    requests, positions, columns = latent_cache.shape
    model = residual.shape[1]
    bf16 = jnp.bfloat16
    shape = jax.ShapeDtypeStruct
    reach = max(1, count // 2)

    id_rows = -(-tokens * TOPK // 1024) * 8
    flat_ids = jnp.pad(expert_ids.reshape(-1), (0, id_rows * 128 - tokens * TOPK))
    rows, values, all_ids = vmem_call(
        functools.partial(gather_kernel, count),
        (
            shape((requests, 2, positions, columns), bf16),
            shape((value_proj.shape[0], count) + value_proj.shape[1:], bf16),
            shape((count, id_rows, 128), jnp.int32),
        ),
        [
            dma(), dma(), dma(2, reach), dma(2, reach), dma(count - 1), dma(count - 1), dma(3),
        ],
        0,
        latent_cache, value_proj, flat_ids.reshape(id_rows, 128),
    )
    scores, flat_rows = masked_scores(
        queries, rows.reshape(requests, 2 * positions, columns), token_request, token_visible
    )
    summed, totals = weighted_rows(scores, jnp.max(scores, axis=2), flat_rows)
    context = (summed / totals[:, :, None]).astype(bf16)
    head_values = jnp.einsum(
        "thl,hlv->thv",
        context,
        values.reshape(heads, LATENT, VDIM),
        preferred_element_type=jnp.float32,
    )
    heads_out = head_values.astype(bf16).reshape(tokens, heads * VDIM)
    width = out_proj.shape[1]
    normed, hidden = vmem_call(
        functools.partial(middle_kernel, count),
        (shape((count, 2, half, model), bf16), shape((2, half, model // 2), bf16)),
        [
            pltpu.VMEM((count, tokens, heads * VDIM), bf16),
            pltpu.VMEM((count, 2, half, width), jnp.float32),
            pltpu.VMEM((count, half, width), jnp.float32),
            pltpu.VMEM((count - 1, half, width), bf16),
            pltpu.VMEM((count, half, width), bf16),
            pltpu.VMEM((2, half, model // 2), bf16),
            pltpu.VMEM((half, model), bf16),
            dma(2, reach), dma(2, reach), dma(count), dma(count), dma(count - 1), dma(count - 1),
            dma(2, reach), dma(2, reach), dma(count), dma(count), dma(2), dma(), dma(),
        ],
        1,
        heads_out,
        out_proj,
        lax.dynamic_slice_in_dim(residual, core * half, half, 0),
        norm_gain.reshape(1, model),
    )
    normed = normed.reshape(count * tokens, model)

    local = EXPERTS // count
    ids = all_ids.reshape(count, -1)[:, : tokens * TOPK].reshape(count * tokens, TOPK)
    named = jnp.any(ids[:, :, None] == jnp.arange(EXPERTS, dtype=jnp.int32), axis=1)
    logits = jnp.dot(normed, router, preferred_element_type=jnp.float32)
    logits = jnp.where(named, logits, -jnp.inf)
    raised = jnp.exp(logits - jnp.max(logits, axis=1, keepdims=True))
    share = (raised / jnp.sum(raised, axis=1, keepdims=True)).astype(bf16)
    first = me * local
    here = lax.dynamic_slice_in_dim(named, first, local, 1)
    share_here = lax.dynamic_slice_in_dim(share, first, local, 1)
    before = jnp.tril(jnp.ones((tokens, tokens), bf16), -1)
    ranks = jnp.einsum(
        "st,bte->bse",
        before,
        here.reshape(count, tokens, local).astype(bf16),
        preferred_element_type=jnp.float32,
    ).astype(jnp.int32)
    source = jnp.arange(count, dtype=jnp.int32)
    place = (ranks + source[:, None, None] * CAP).reshape(count * tokens, local)
    hits = here[:, :, None] & (place[:, :, None] == jnp.arange(count * CAP, dtype=jnp.int32))
    mixing = jnp.where(hits, share_here[:, :, None], jnp.zeros((), bf16))
    picked = jnp.einsum(
        "tes,td->esd", hits.astype(bf16), normed, preferred_element_type=jnp.float32
    ).astype(bf16)

    slots = count * CAP
    blocks = gate_weight.shape[0] // local
    hidden_here = gate_weight.shape[2]
    expert_rows = pl.pallas_call(
        functools.partial(expert_kernel, blocks),
        grid=(local,),
        out_shape=shape((local, slots, model), bf16),
        in_specs=[
            pl.BlockSpec((1, slots, model), lambda e: (e, 0, 0)),
            pl.BlockSpec((blocks, model, hidden_here), lambda e: (e, 0, 0)),
            pl.BlockSpec((blocks, model, hidden_here), lambda e: (e, 0, 0)),
            pl.BlockSpec((blocks, hidden_here, model), lambda e: (e, 0, 0)),
        ],
        out_specs=pl.BlockSpec((1, slots, model), lambda e: (e, 0, 0)),
        compiler_params=pltpu.CompilerParams(vmem_limit_bytes=40 * 2**20),
    )(picked, gate_weight, up_weight, down_weight)
    sums = [
        jnp.einsum(
            "tes,esd->td",
            mixing,
            expert_rows[:, :, side * (model // 2) : (side + 1) * (model // 2)],
            preferred_element_type=jnp.float32,
        ).astype(bf16)
        for side in range(2)
    ]
    sums = jnp.stack(sums).reshape(2, count, tokens, model // 2)
    block = (tokens, model // 2)
    expert_out = vmem_call(
        functools.partial(return_kernel, count),
        shape(block, bf16),
        [
            pltpu.VMEM((count,) + block, bf16),
            pltpu.VMEM((count - 1,) + block, bf16),
            pltpu.VMEM((count - 1,) + block, bf16),
            dma(count), dma(count), dma(count - 1), dma(count - 1),
        ],
        2,
        sums,
    )
    return (hidden.reshape(tokens, model // 2), expert_out)


LEAN_BYTES = 8 * 2**20


def choose(mesh):
    count = mesh.shape["ep"]

    def layer(*args):
        tokens, model = args[2].shape
        fits = count * tokens * model * 2 <= LEAN_BYTES
        even = count % 2 == 0 and tokens % 32 == 0 and EXPERTS % count == 0
        if fits and even and mesh.shape["tp"] == 2:
            return lean_body(*args)
        return body(*args)

    return layer


def solution(mesh):
    return jax.shard_map(
        choose(mesh),
        mesh=mesh,
        in_specs=(
            P(("grp", "ep"), "tp", None),
            P(("grp", "ep"), "tp", None),
            P(("grp", "ep"), None),
            P(("grp", "ep")),
            P(("grp", "ep")),
            P("tp", "ep", None),
            P("tp", "ep"),
            P(),
            P(),
            P(("grp", "ep"), None),
            P("ep", None, "tp"),
            P("ep", None, "tp"),
            P("ep", "tp", None),
        ),
        out_specs=(P(("grp", "ep"), "tp"), P(("grp", "ep"), "tp")),
        check_vma=False,
    )
```

```python
import functools

import jax
import jax.numpy as jnp
from jax import lax
from jax.experimental import pallas as pl
from jax.experimental.pallas import tpu as pltpu
from jax.sharding import PartitionSpec as P

LATENT = 512
VDIM = 128
EXPERTS = 64
TOPK = 6
GROUPS = 2
CAP = 8
PIECES = 128
MESH = pl.DeviceIdType.MESH


score_scale = 192.0 ** (-0.5)
epsilon = 1e-06


def masked_scores(queries, block_rows, token_request, token_visible):
    per_request = block_rows.shape[1]
    flat_rows = block_rows.reshape(-1, block_rows.shape[2])
    scores = (
        jnp.einsum("thc,kc->thk", queries, flat_rows, preferred_element_type=jnp.float32)
        * score_scale
    )
    column = jnp.arange(flat_rows.shape[0], dtype=jnp.int32)
    owner_id = column // per_request
    position = column % per_request
    allowed = (owner_id[None, :] == token_request[:, None]) & (
        position[None, :] < token_visible[:, None]
    )
    return (jnp.where(allowed[:, None, :], scores, -jnp.inf), flat_rows)


def weighted_rows(scores, row_peak, flat_rows):
    weights = jnp.exp(scores - row_peak[:, :, None]).astype(jnp.bfloat16)
    totals = jnp.sum(weights.astype(jnp.float32), axis=2)
    summed = jnp.einsum(
        "thk,kc->thc", weights, flat_rows[:, :LATENT], preferred_element_type=jnp.float32
    )
    return (summed, totals)


def expert_block(arrived, gate_weight, up_weight, down_weight):
    gate_vals = jnp.einsum("prd,pdf->prf", arrived, gate_weight, preferred_element_type=jnp.float32)
    up_vals = jnp.einsum("prd,pdf->prf", arrived, up_weight, preferred_element_type=jnp.float32)
    activated = (jax.nn.silu(gate_vals) * up_vals).astype(jnp.bfloat16)
    return jnp.einsum(
        "prf,pfd->prd", activated, down_weight, preferred_element_type=jnp.float32
    ).astype(jnp.bfloat16)


def body(
    queries,
    latent_cache,
    residual,
    token_request,
    token_visible,
    value_proj,
    out_proj,
    norm_gain,
    router,
    expert_ids,
    gate_weight,
    up_weight,
    down_weight,
):
    all_rows = lax.all_gather(latent_cache, "tp", axis=1, tiled=True)
    scores, flat_rows = masked_scores(queries, all_rows, token_request, token_visible)
    summed, totals = weighted_rows(scores, jnp.max(scores, axis=2), flat_rows)
    context = (summed / totals[:, :, None]).astype(jnp.bfloat16)
    tokens_here = context.shape[0]
    heads_here = context.shape[1]
    head_values = jnp.einsum(
        "thl,hlv->thv",
        context,
        lax.all_gather(value_proj, "ep", axis=1, tiled=True),
        preferred_element_type=jnp.float32,
    )
    heads_out = head_values.astype(jnp.bfloat16).reshape(tokens_here, heads_here * VDIM)
    column_block = jnp.dot(
        lax.all_gather(heads_out, "ep", axis=0, tiled=True),
        out_proj,
        preferred_element_type=jnp.float32,
    )
    attention_part = lax.all_to_all(column_block, "ep", split_axis=0, concat_axis=1, tiled=True)
    attention = lax.psum(attention_part, "tp")
    hidden = (residual.astype(jnp.float32) + attention).astype(jnp.bfloat16)
    hidden_wide = hidden.astype(jnp.float32)
    normed = (
        hidden_wide
        * lax.rsqrt(jnp.mean(hidden_wide * hidden_wide, axis=1, keepdims=True) + epsilon)
        * norm_gain
    ).astype(jnp.bfloat16)
    logits = jnp.dot(normed, router, preferred_element_type=jnp.float32)
    gate_share = jax.nn.softmax(jnp.take_along_axis(logits, expert_ids, axis=1), axis=1).astype(
        jnp.bfloat16
    )
    flat_ids = expert_ids.reshape(-1)
    position_id = jnp.arange(flat_ids.shape[0], dtype=jnp.int32)
    earlier = (flat_ids[:, None] == flat_ids[None, :]) & (
        position_id[None, :] < position_id[:, None]
    )
    slot_ids = (flat_ids * CAP + jnp.sum(earlier.astype(jnp.int32), axis=1)).reshape(
        tokens_here, TOPK
    )
    targets = jnp.arange(EXPERTS * CAP, dtype=jnp.int32)
    matches = slot_ids[:, :, None] == targets[None, None, :]
    picker = jnp.any(matches, axis=1).T.astype(jnp.bfloat16)
    model_width = normed.shape[1]
    mixing = jnp.sum(
        jnp.where(matches, gate_share[:, :, None], jnp.zeros((), jnp.bfloat16)), axis=1
    )
    mixing = jnp.broadcast_to(
        mixing.reshape(tokens_here, EXPERTS, 1, CAP), (tokens_here, EXPERTS, GROUPS, CAP)
    ).reshape(tokens_here, PIECES * CAP)
    core_count = lax.axis_size("tp")
    half_width = model_width // core_count
    core_start = lax.axis_index("tp") * half_width
    outgoing = jnp.dot(picker, normed, preferred_element_type=jnp.float32).astype(jnp.bfloat16)
    outgoing = jnp.broadcast_to(
        outgoing.reshape(EXPERTS, 1, CAP, model_width), (EXPERTS, GROUPS, CAP, model_width)
    ).reshape(PIECES, CAP, model_width)
    arrived = lax.all_to_all(outgoing, "ep", split_axis=0, concat_axis=1, tiled=True)
    partial_out = expert_block(arrived, gate_weight, up_weight, down_weight)
    returned = lax.all_to_all(partial_out, "ep", split_axis=1, concat_axis=0, tiled=True)
    routed = jnp.dot(
        mixing, returned.reshape(PIECES * CAP, model_width), preferred_element_type=jnp.float32
    )
    expert_out = lax.psum_scatter(
        routed.astype(jnp.bfloat16), "tp", scatter_dimension=1, tiled=True
    )
    hidden_part = lax.dynamic_slice_in_dim(hidden, core_start, half_width, 1)
    return (hidden_part, expert_out)


def ring_position(index, count):
    half = lax.div(index, 2)
    return half + lax.rem(index, 2) * (count - 1 - 2 * half)


def ring_index(place, count):
    place = lax.rem(place + count, count)
    upper = lax.div(place, count // 2)
    return 2 * place + upper * (2 * count - 1 - 4 * place)


def greet(count):
    me = lax.axis_index("ep")
    core = lax.axis_index("tp")
    barrier = pltpu.get_barrier_semaphore()
    for step in range(1, count):
        pl.semaphore_signal(
            barrier, inc=1, device_id={"ep": lax.rem(me + step, count)}, device_id_type=MESH
        )
    pl.semaphore_signal(barrier, inc=1, device_id={"tp": 1 - core}, device_id_type=MESH)
    pl.semaphore_wait(barrier, count)


def remote(src, dst, send_sem, recv_sem, where):
    return pltpu.make_async_remote_copy(
        src_ref=src,
        dst_ref=dst,
        send_sem=send_sem,
        recv_sem=recv_sem,
        device_id=where,
        device_id_type=MESH,
    )


def ring_gather(count, own, slot, send_sem, recv_sem, arrived):
    me = lax.axis_index("ep")
    place = ring_position(me, count)
    far = count // 2
    near = count - 1 - far
    to = (ring_index(place + 1, count), ring_index(place - 1, count))

    def reach(way, part):
        return far if way == part else near

    def origin(way, step):
        return ring_index(place - step if way == 0 else place + step, count)

    hops = {}

    def hop(way, step, part):
        if step > reach(way, part):
            return
        block = origin(way, step - 1)
        hops[way, step, part] = remote(
            own(part) if step == 1 else slot(block, part),
            slot(block, part),
            send_sem.at[way, step - 1, part],
            recv_sem.at[way, step - 1, part],
            {"ep": to[way]},
        )
        hops[way, step, part].start()

    for turn in range(2):
        for way in range(2):
            hop(way, 1, (way + turn) % 2)
    arrived(me, 0)
    number = 1
    for step in range(1, far + 1):
        for turn in range(2):
            for way in range(2):
                part = (way + turn) % 2
                if step <= reach(way, part):
                    hops[way, step, part].wait_recv()
                    hop(way, step + 1, part)
        for way in range(2 if step <= near else 1):
            arrived(origin(way, step), number)
            number += 1
    for copy in hops.values():
        copy.wait_send()


def gather_kernel(
    count, cache_ref, value_ref, ids_ref, rows_ref, values_ref, all_ids_ref,
    tp_send, tp_recv, ring_send, ring_recv, id_send, id_recv, own_sem,
):
    me = lax.axis_index("ep")
    core = lax.axis_index("tp")
    some = value_ref.shape[0] // 2
    greet(count)
    swap = remote(cache_ref, rows_ref.at[:, core], tp_send, tp_recv, {"tp": 1 - core})
    swap.start()
    owns = [
        pltpu.make_async_copy(cache_ref, rows_ref.at[:, core], own_sem.at[0]),
        pltpu.make_async_copy(value_ref, values_ref.at[:, me], own_sem.at[1]),
        pltpu.make_async_copy(ids_ref, all_ids_ref.at[me], own_sem.at[2]),
    ]
    for copy in owns:
        copy.start()
    id_copies = [
        remote(
            ids_ref, all_ids_ref.at[me], id_send.at[step - 1], id_recv.at[step - 1],
            {"ep": lax.rem(me + step, count)},
        )
        for step in range(1, count)
    ]
    for copy in id_copies:
        copy.start()
    ring_gather(
        count,
        lambda part: value_ref.at[pl.ds(part * some, some)],
        lambda block, part: values_ref.at[pl.ds(part * some, some), block],
        ring_send,
        ring_recv,
        lambda block, number: None,
    )
    for copy in id_copies:
        copy.wait()
    for copy in owns:
        copy.wait()
    swap.wait()


def middle_kernel(
    count, heads_ref, proj_ref, residual_ref, gain_ref, normed_ref, hidden_ref,
    gathered, mine, theirs, outbox, inbox, hidden_own, normed_own,
    ring_send, ring_recv, pair_send, pair_recv, back_send, back_recv,
    ring2_send, ring2_recv, fwd_send, fwd_recv, own_sem, swap_send, swap_recv,
):
    me = lax.axis_index("ep")
    core = lax.axis_index("tp")
    tokens = heads_ref.shape[0]
    half = tokens // 2
    width = proj_ref.shape[1]
    model = residual_ref.shape[1]
    greet(count)
    pairs = []

    def project(block, number):
        rows = heads_ref[...] if number == 0 else gathered[block]
        product = jnp.dot(rows, proj_ref[...], preferred_element_type=jnp.float32)
        mine[number] = product.reshape(2, half, width)
        copy = remote(
            mine.at[number, 1 - core], theirs.at[number], pair_send.at[number],
            pair_recv.at[number], {"tp": 1 - core},
        )
        copy.start()
        pairs.append((copy, block))

    backs = []

    def pass_back(number):
        copy, block = pairs[number]
        copy.wait_recv()
        total = (mine[number, core] + theirs[number]).astype(jnp.bfloat16)
        if number == 0:
            inbox[me] = total
        else:
            outbox[number - 1] = total
            back = remote(
                outbox.at[number - 1], inbox.at[me], back_send.at[number - 1],
                back_recv.at[number - 1], {"ep": block},
            )
            back.start()
            backs.append(back)

    def arrived(block, number):
        project(block, number)
        if number >= 1:
            pass_back(number - 1)

    ring_gather(
        count,
        lambda part: heads_ref.at[pl.ds(part * half, half)],
        lambda block, part: gathered.at[block, pl.ds(part * half, half)],
        ring_send,
        ring_recv,
        arrived,
    )
    pass_back(count - 1)
    for copy, _ in pairs:
        copy.wait_send()
    for back in backs:
        back.wait()
    attention = jnp.concatenate([inbox[i] for i in range(count)], axis=1).astype(jnp.float32)
    hidden = (residual_ref[...].astype(jnp.float32) + attention).astype(jnp.bfloat16)
    wide = hidden.astype(jnp.float32)
    scale = lax.rsqrt(jnp.mean(wide * wide, axis=1, keepdims=True) + epsilon)
    normed_own[...] = (wide * scale * gain_ref[...]).astype(jnp.bfloat16)
    hidden_own[0] = hidden[:, : model // 2]
    hidden_own[1] = hidden[:, model // 2 :]
    swap = remote(
        hidden_own.at[1 - core], hidden_ref.at[core], swap_send, swap_recv, {"tp": 1 - core}
    )
    swap.start()
    owns = [
        pltpu.make_async_copy(hidden_own.at[core], hidden_ref.at[core], own_sem.at[0]),
        pltpu.make_async_copy(normed_own, normed_ref.at[me, core], own_sem.at[1]),
    ]
    for copy in owns:
        copy.start()
    forwards = []

    def forward(block, number):
        source = normed_own if number == 0 else normed_ref.at[block, core]
        copy = remote(
            source, normed_ref.at[block, core], fwd_send.at[number], fwd_recv.at[number],
            {"tp": 1 - core},
        )
        copy.start()
        forwards.append(copy)

    some = half // 2
    ring_gather(
        count,
        lambda part: normed_own.at[pl.ds(part * some, some)],
        lambda block, part: normed_ref.at[block, core, pl.ds(part * some, some)],
        ring2_send,
        ring2_recv,
        forward,
    )
    for copy in forwards:
        copy.wait()
    for copy in owns:
        copy.wait()
    swap.wait()


def return_kernel(
    count, sums_ref, out_ref, theirs, outbox, inbox, outbox2, inbox2,
    pair_send, pair_recv, cross_send, cross_recv, back_send, back_recv,
):
    me = lax.axis_index("ep")
    core = lax.axis_index("tp")
    half = count // 2
    twin = me + 1 - 2 * lax.rem(me, 2)
    greet(count)
    steps = list(range(1, half)) + [0]
    order = [lax.rem(start + 2 * step, count) for start in (twin, me) for step in steps]
    pairs = []
    for number, block in enumerate(order):
        copy = remote(
            sums_ref.at[1 - core, block], theirs.at[number], pair_send.at[number],
            pair_recv.at[number], {"tp": 1 - core},
        )
        copy.start()
        pairs.append(copy)

    def both(number):
        pairs[number].wait_recv()
        return sums_ref[core, order[number]].astype(jnp.float32) + theirs[number].astype(
            jnp.float32
        )

    crosses = []
    for number in range(half):
        outbox[number] = both(number).astype(jnp.bfloat16)
        cross = remote(
            outbox.at[number], inbox.at[number], cross_send.at[number], cross_recv.at[number],
            {"ep": twin},
        )
        cross.start()
        crosses.append(cross)
    backs = []
    for number in range(half):
        total = both(half + number)
        crosses[number].wait_recv()
        total = total + inbox[number].astype(jnp.float32)
        if number < half - 1:
            outbox2[number] = total.astype(jnp.bfloat16)
            back = remote(
                outbox2.at[number], inbox2.at[number], back_send.at[number],
                back_recv.at[number], {"ep": order[half + number]},
            )
            back.start()
            backs.append(back)
    for number, back in enumerate(backs):
        back.wait_recv()
        total = total + inbox2[number].astype(jnp.float32)
    out_ref[...] = total.astype(jnp.bfloat16)
    for copy in pairs + crosses + backs:
        copy.wait_send()


def expert_kernel(blocks, rows_ref, gate_ref, up_ref, down_ref, out_ref):
    rows = rows_ref[0]
    total = None
    for block in range(blocks):
        gate = lax.dot_general(
            rows, gate_ref[block], (((1,), (1,)), ((), ())), preferred_element_type=jnp.float32
        )
        up = lax.dot_general(
            rows, up_ref[block], (((1,), (1,)), ((), ())), preferred_element_type=jnp.float32
        )
        activated = (gate / (1.0 + jnp.exp(-gate)) * up).astype(jnp.bfloat16)
        part = jnp.dot(activated, down_ref[block], preferred_element_type=jnp.float32)
        total = part if total is None else total + part
    out_ref[0] = total.astype(jnp.bfloat16)


def vmem_call(kernel, outs, scratch, ident, *args):
    whole = pl.BlockSpec(memory_space=pltpu.VMEM)
    return pl.pallas_call(
        kernel,
        out_shape=outs,
        in_specs=[whole] * len(args),
        out_specs=jax.tree.map(lambda _: whole, outs),
        scratch_shapes=scratch,
        compiler_params=pltpu.CompilerParams(
            collective_id=ident, has_side_effects=True, vmem_limit_bytes=40 * 2**20
        ),
    )(*args)


def dma(*shape):
    return pltpu.SemaphoreType.DMA(shape)


def lean_body(
    queries,
    latent_cache,
    residual,
    token_request,
    token_visible,
    value_proj,
    out_proj,
    norm_gain,
    router,
    expert_ids,
    gate_weight,
    up_weight,
    down_weight,
):
    count = lax.axis_size("ep")
    core = lax.axis_index("tp")
    me = lax.axis_index("ep")
    tokens, heads = queries.shape[:2]
    half = tokens // 2
    requests, positions, columns = latent_cache.shape
    model = residual.shape[1]
    bf16 = jnp.bfloat16
    shape = jax.ShapeDtypeStruct
    reach = max(1, count // 2)

    id_rows = -(-tokens * TOPK // 1024) * 8
    flat_ids = jnp.pad(expert_ids.reshape(-1), (0, id_rows * 128 - tokens * TOPK))
    rows, values, all_ids = vmem_call(
        functools.partial(gather_kernel, count),
        (
            shape((requests, 2, positions, columns), bf16),
            shape((value_proj.shape[0], count) + value_proj.shape[1:], bf16),
            shape((count, id_rows, 128), jnp.int32),
        ),
        [
            dma(), dma(), dma(2, reach, 2), dma(2, reach, 2), dma(count - 1), dma(count - 1), dma(3),
        ],
        0,
        latent_cache, value_proj, flat_ids.reshape(id_rows, 128),
    )
    scores, flat_rows = masked_scores(
        queries, rows.reshape(requests, 2 * positions, columns), token_request, token_visible
    )
    summed, totals = weighted_rows(scores, jnp.max(scores, axis=2), flat_rows)
    context = (summed / totals[:, :, None]).astype(bf16)
    head_values = jnp.einsum(
        "thl,hlv->thv",
        context,
        values.reshape(heads, LATENT, VDIM),
        preferred_element_type=jnp.float32,
    )
    heads_out = head_values.astype(bf16).reshape(tokens, heads * VDIM)
    width = out_proj.shape[1]
    normed, hidden = vmem_call(
        functools.partial(middle_kernel, count),
        (shape((count, 2, half, model), bf16), shape((2, half, model // 2), bf16)),
        [
            pltpu.VMEM((count, tokens, heads * VDIM), bf16),
            pltpu.VMEM((count, 2, half, width), jnp.float32),
            pltpu.VMEM((count, half, width), jnp.float32),
            pltpu.VMEM((count - 1, half, width), bf16),
            pltpu.VMEM((count, half, width), bf16),
            pltpu.VMEM((2, half, model // 2), bf16),
            pltpu.VMEM((half, model), bf16),
            dma(2, reach, 2), dma(2, reach, 2), dma(count), dma(count), dma(count - 1), dma(count - 1),
            dma(2, reach, 2), dma(2, reach, 2), dma(count), dma(count), dma(2), dma(), dma(),
        ],
        1,
        heads_out,
        out_proj,
        lax.dynamic_slice_in_dim(residual, core * half, half, 0),
        norm_gain.reshape(1, model),
    )
    normed = normed.reshape(count * tokens, model)

    local = EXPERTS // count
    ids = all_ids.reshape(count, -1)[:, : tokens * TOPK].reshape(count * tokens, TOPK)
    named = jnp.any(ids[:, :, None] == jnp.arange(EXPERTS, dtype=jnp.int32), axis=1)
    logits = jnp.dot(normed, router, preferred_element_type=jnp.float32)
    logits = jnp.where(named, logits, -jnp.inf)
    raised = jnp.exp(logits - jnp.max(logits, axis=1, keepdims=True))
    share = (raised / jnp.sum(raised, axis=1, keepdims=True)).astype(bf16)
    first = me * local
    here = lax.dynamic_slice_in_dim(named, first, local, 1)
    share_here = lax.dynamic_slice_in_dim(share, first, local, 1)
    before = jnp.tril(jnp.ones((tokens, tokens), bf16), -1)
    ranks = jnp.einsum(
        "st,bte->bse",
        before,
        here.reshape(count, tokens, local).astype(bf16),
        preferred_element_type=jnp.float32,
    ).astype(jnp.int32)
    source = jnp.arange(count, dtype=jnp.int32)
    place = (ranks + source[:, None, None] * CAP).reshape(count * tokens, local)
    hits = here[:, :, None] & (place[:, :, None] == jnp.arange(count * CAP, dtype=jnp.int32))
    mixing = jnp.where(hits, share_here[:, :, None], jnp.zeros((), bf16))
    picked = jnp.einsum(
        "tes,td->esd", hits.astype(bf16), normed, preferred_element_type=jnp.float32
    ).astype(bf16)

    slots = count * CAP
    blocks = gate_weight.shape[0] // local
    hidden_here = gate_weight.shape[2]
    expert_rows = pl.pallas_call(
        functools.partial(expert_kernel, blocks),
        grid=(local,),
        out_shape=shape((local, slots, model), bf16),
        in_specs=[
            pl.BlockSpec((1, slots, model), lambda e: (e, 0, 0)),
            pl.BlockSpec((blocks, hidden_here, model), lambda e: (e, 0, 0)),
            pl.BlockSpec((blocks, hidden_here, model), lambda e: (e, 0, 0)),
            pl.BlockSpec((blocks, hidden_here, model), lambda e: (e, 0, 0)),
        ],
        out_specs=pl.BlockSpec((1, slots, model), lambda e: (e, 0, 0)),
        compiler_params=pltpu.CompilerParams(vmem_limit_bytes=40 * 2**20),
    )(picked, jnp.swapaxes(gate_weight, 1, 2), jnp.swapaxes(up_weight, 1, 2), down_weight)
    sums = [
        jnp.einsum(
            "tes,esd->td",
            mixing,
            expert_rows[:, :, side * (model // 2) : (side + 1) * (model // 2)],
            preferred_element_type=jnp.float32,
        ).astype(bf16)
        for side in range(2)
    ]
    sums = jnp.stack(sums).reshape(2, count, tokens, model // 2)
    block = (tokens, model // 2)
    expert_out = vmem_call(
        functools.partial(return_kernel, count),
        shape(block, bf16),
        [
            pltpu.VMEM((count,) + block, bf16),
            pltpu.VMEM((reach,) + block, bf16),
            pltpu.VMEM((reach,) + block, bf16),
            pltpu.VMEM((reach - 1,) + block, bf16),
            pltpu.VMEM((reach - 1,) + block, bf16),
            dma(count), dma(count), dma(reach), dma(reach), dma(reach - 1), dma(reach - 1),
        ],
        2,
        sums,
    )
    return (hidden.reshape(tokens, model // 2), expert_out)


LEAN_BYTES = 8 * 2**20


def choose(mesh):
    count = mesh.shape["ep"]

    def layer(*args):
        tokens, model = args[2].shape
        fits = count * tokens * model * 2 <= LEAN_BYTES
        even = count % 2 == 0 and count >= 4 and tokens % 32 == 0 and EXPERTS % count == 0
        if fits and even and mesh.shape["tp"] == 2:
            return lean_body(*args)
        return body(*args)

    return layer


def solution(mesh):
    return jax.shard_map(
        choose(mesh),
        mesh=mesh,
        in_specs=(
            P(("grp", "ep"), "tp", None),
            P(("grp", "ep"), "tp", None),
            P(("grp", "ep"), None),
            P(("grp", "ep")),
            P(("grp", "ep")),
            P("tp", "ep", None),
            P("tp", "ep"),
            P(),
            P(),
            P(("grp", "ep"), None),
            P("ep", None, "tp"),
            P("ep", None, "tp"),
            P("ep", "tp", None),
        ),
        out_specs=(P(("grp", "ep"), "tp"), P(("grp", "ep"), "tp")),
        check_vma=False,
    )
```
